768 devices in a mesh: worker: 16 (over x, y_lo, core), fsdp: 48 (over y_hi, z).
Axes of the slice: x: 4, y: 8 (y_hi: 4, y_lo: 2; y = y_hi * 2 + y_lo), z: 12, core: 2. Of those that a mesh axis runs over, the one named last changes fastest.
Arguments:
- queries: bfloat16 [196608, 2048], P(('worker', 'fsdp')), may hold values from -52 to 52
- key_states: bfloat16 [196608, 512], P(('worker', 'fsdp')), may hold values from -6 to 6
- value_states: bfloat16 [196608, 512], P(('worker', 'fsdp')), may hold values from -6 to 6
- output_grad: bfloat16 [196608, 2048], P(('worker', 'fsdp')), may hold values from -6 to 6
- key_blocks: int32 [1536, 2], P(('worker', 'fsdp')), may hold values from 0 to 15, as said below
- global_params: float32 [2, 3145728], P(None, 'fsdp'), may hold values from -6 to 6
- local_params: float32 [16, 3145728], P('worker', 'fsdp'), may hold values from -6 to 6
- momentum: float32 [2, 48, 16, 4096], P(None, 'fsdp', 'worker'), may hold values from -3 to 3
- fragment: int32 [1], replicated, may hold values from 0 to 1
Outputs:
- query_grad: bfloat16 [196608, 2048], P(('worker', 'fsdp'))
- key_grad: bfloat16 [196608, 512], P(('worker', 'fsdp'))
- value_grad: bfloat16 [196608, 512], P(('worker', 'fsdp'))
- new_params: float32 [2, 3145728], P(None, 'fsdp')
- new_momentum: float32 [2, 48, 16, 4096], P(None, 'fsdp', 'worker')
The draws below stay inside these ranges and needn't reach their ends.
Inputs may be any that keep to these rules, and one draw needn't show every extreme that they name: `key_blocks`: entry 0 of each row is the row's own block index within its sequence; entry 1 is that index or the one before it.
All inputs are finite; a program needn't handle non-finite values.
Results may differ from the reference program's by a relative error of at most 0.005.
Values may be sent and summed in bfloat16 or wider, within the bound.
No kernel may reach another device: no remote copies, remote signals or barrier semaphores. Data moves between devices by JAX's collectives and lax.ppermute only.
A program may use at most 32 MiB of HBM per device.

```python
import math
import jax
import jax.numpy as jnp
from jax import lax

HEADS = 16
KV_HEADS = 4
HEAD_DIM = 128
BLOCK = 128
LENGTH = 2048
PICK = 2
FRAGS = 2
FRAG_DEV = 65536
TOKENS = 196608
FRAG = 3145728
N_WORKER = 16
N_FSDP = 48


def query_key_pair(key):
    base = jax.random.fold_in(key, 4242)
    query_key, state_key = jax.random.split(base, 2)
    groups = HEADS // KV_HEADS
    query_draw = jnp.clip(jax.random.normal(query_key, (TOKENS, KV_HEADS, groups, HEAD_DIM), jnp.float32), -6.0, 6.0)
    key_draw = jnp.clip(jax.random.normal(state_key, (TOKENS, KV_HEADS, HEAD_DIM), jnp.float32), -6.0, 6.0)
    return (query_draw.reshape(TOKENS, HEADS * HEAD_DIM), key_draw.reshape(TOKENS, KV_HEADS * HEAD_DIM))


def draw_queries(key, part):
    return query_key_pair(key)[0].astype(jnp.bfloat16)


def draw_key_states(key, part):
    return query_key_pair(key)[1].astype(jnp.bfloat16)


def draw_key_blocks(key, part):
    block_rows = TOKENS // BLOCK
    own_block = jnp.arange(block_rows, dtype=jnp.int32) % (LENGTH // BLOCK)
    backward = jax.random.randint(jax.random.fold_in(key, 77), (block_rows,), 0, 2, dtype=jnp.int32)
    other_block = jnp.maximum(own_block - backward, 0)
    return jnp.stack([own_block, other_block], 1)


def steps_of(key, extent, cuts, smallest, largest):
    loudness = 1.0
    for dim, blocks in cuts:
        steps = jax.random.uniform(jax.random.fold_in(jax.random.fold_in(key, 6), dim), (blocks,), jnp.float32, smallest / len(cuts), largest / len(cuts))
        loudness = loudness * jnp.repeat(jnp.exp(steps), extent[dim] // blocks).reshape((-1,) + (1,) * (len(extent) - 1 - dim))
    return loudness


def normal_values(stream_key, dims, scale, limit, cuts=(), kind=jnp.bfloat16):
    result = jax.random.normal(stream_key, dims, jnp.float32) * scale
    if len(cuts) > 0:
        result = steps_of(stream_key, dims, cuts, -0.22, 0.18) * result
    return jnp.clip(result, min=-limit, max=limit).astype(kind)


def setup_inputs(seed: int = 0) -> dict:
    arg_keys = jax.random.split(jax.random.key(seed), 10)
    return {
        "queries": draw_queries(jax.random.fold_in(arg_keys[9], 71), 0),
        "key_states": draw_key_states(jax.random.fold_in(arg_keys[9], 71), 0),
        "value_states": normal_values(arg_keys[2], (TOKENS, KV_HEADS * HEAD_DIM), 1.0, 6.0, ((0, 768),)),
        "output_grad": normal_values(arg_keys[3], (TOKENS, HEADS * HEAD_DIM), 1.0, 6.0, ((0, 768),)),
        "key_blocks": draw_key_blocks(jax.random.fold_in(arg_keys[9], 71), 0),
        "global_params": normal_values(arg_keys[5], (FRAGS, FRAG), 1.0, 6.0, ((1, 48),), jnp.float32),
        "local_params": normal_values(arg_keys[6], (N_WORKER, FRAG), 1.0, 6.0, ((0, 16), (1, 48)), jnp.float32),
        "momentum": normal_values(arg_keys[7], (FRAGS, N_FSDP, N_WORKER, FRAG_DEV // N_WORKER), 0.5, 3.0, ((1, 48), (2, 16)), jnp.float32),
        "fragment": jax.random.randint(arg_keys[8], (1,), 0, FRAGS).astype(jnp.int32),
    }


outer_rate = 0.7
outer_moment = 0.9

def sequence_grads(packed):
    seq_queries, seq_keys, seq_values, seq_grad, seq_blocks = packed
    blocks = LENGTH // BLOCK
    groups = HEADS // KV_HEADS
    scaling = 1.0 / math.sqrt(HEAD_DIM)
    width = KV_HEADS * HEAD_DIM
    query_heads = seq_queries.astype(jnp.float32).reshape(blocks, BLOCK, KV_HEADS, groups, HEAD_DIM)
    grad_heads = seq_grad.astype(jnp.float32).reshape(blocks, BLOCK, KV_HEADS, groups, HEAD_DIM)

    def window(states):
        padded = jnp.concatenate([jnp.zeros((BLOCK, width), states.dtype), states], 0)
        padded = padded.astype(jnp.float32).reshape(blocks + 1, BLOCK, KV_HEADS, HEAD_DIM)
        return jnp.concatenate([padded[:blocks], padded[1:]], 1)
    key_window = window(seq_keys)
    value_window = window(seq_values)
    block_ids = jnp.arange(blocks, dtype=jnp.int32)
    slot_ids = jnp.arange(2 * BLOCK, dtype=jnp.int32)
    key_block = block_ids[:, None] - 1 + slot_ids[None, :] // BLOCK
    key_place = key_block * BLOCK + slot_ids[None, :] % BLOCK
    query_place = block_ids[:, None] * BLOCK + jnp.arange(BLOCK, dtype=jnp.int32)[None, :]
    chosen = (key_block[:, None, :] == seq_blocks[:, 0][:, None, None]) | (key_block[:, None, :] == seq_blocks[:, 1][:, None, None])
    allowed = chosen & (key_place[:, None, :] <= query_place[:, :, None])
    scores = jnp.einsum('nbgrd,nsgd->ngrbs', query_heads, key_window) * scaling
    scores = jnp.where(allowed[:, None, None], scores, -jnp.inf)
    row_top = lax.optimization_barrier(jnp.max(scores, -1, keepdims=True))
    log_total = row_top + jnp.log(lax.optimization_barrier(jnp.sum(jnp.exp(scores - row_top), -1, keepdims=True)))
    weights = jnp.exp(scores - log_total)
    weight_grad = jnp.einsum('nbgrd,nsgd->ngrbs', grad_heads, value_window)
    delta = lax.optimization_barrier(jnp.sum(weights * weight_grad, -1, keepdims=True))
    score_grad = lax.optimization_barrier((weights * (weight_grad - delta) * scaling).astype(jnp.bfloat16)).astype(jnp.float32)
    weights_low = lax.optimization_barrier(weights.astype(jnp.bfloat16)).astype(jnp.float32)
    query_grad = jnp.einsum('ngrbs,nsgd->nbgrd', score_grad, key_window).reshape(LENGTH, HEADS * HEAD_DIM).astype(jnp.bfloat16)
    key_part = jnp.einsum('ngrbs,nbgrd->nsgd', score_grad, query_heads)
    value_part = jnp.einsum('ngrbs,nbgrd->nsgd', weights_low, grad_heads)

    def fold(part):
        part = part.reshape(blocks, 2, BLOCK, width)
        later = jnp.concatenate([part[1:, 0], jnp.zeros((1, BLOCK, width), jnp.float32)], 0)
        return (part[:, 1] + later).reshape(LENGTH, width).astype(jnp.bfloat16)
    return (query_grad, fold(key_part), fold(value_part))

def reference(queries, key_states, value_states, output_grad, key_blocks, global_params, local_params, momentum, fragment):
    sequences = TOKENS // LENGTH
    packed = (queries.reshape(sequences, LENGTH, HEADS * HEAD_DIM), key_states.reshape(sequences, LENGTH, KV_HEADS * HEAD_DIM), value_states.reshape(sequences, LENGTH, KV_HEADS * HEAD_DIM), output_grad.reshape(sequences, LENGTH, HEADS * HEAD_DIM), key_blocks.reshape(sequences, LENGTH // BLOCK, PICK))
    query_grad, key_grad, value_grad = lax.map(sequence_grads, packed)
    query_grad = query_grad.reshape(TOKENS, HEADS * HEAD_DIM)
    key_grad = key_grad.reshape(TOKENS, KV_HEADS * HEAD_DIM)
    value_grad = value_grad.reshape(TOKENS, KV_HEADS * HEAD_DIM)
    slot_index = fragment[0]
    current = lax.dynamic_index_in_dim(global_params, slot_index, 0, keepdims=False)
    drift = lax.optimization_barrier(jnp.sum(current[None, :] - local_params, 0)) / N_WORKER
    moment = lax.dynamic_index_in_dim(momentum, slot_index, 0, keepdims=False).reshape(FRAG)
    new_moment = outer_moment * moment + drift
    updated = current - outer_rate * (drift + outer_moment * new_moment)
    new_params = lax.dynamic_update_index_in_dim(global_params, updated, slot_index, 0)
    new_momentum = lax.dynamic_update_index_in_dim(momentum, new_moment.reshape(momentum.shape[1:]), slot_index, 0)
    return (query_grad, key_grad, value_grad, new_params, new_momentum)
```

```python
import math

import jax
import jax.numpy as jnp
from jax import lax
from jax.experimental import pallas as pl
from jax.experimental.pallas import tpu as pltpu
from jax.sharding import PartitionSpec as P

HEADS = 16
KV_HEADS = 4
GROUP = HEADS // KV_HEADS
HEAD_DIM = 128
BLOCK = 128
LENGTH = 2048
LANES = 128

outer_rate = 0.7
outer_moment = 0.9

f32 = jnp.float32
bf16 = jnp.bfloat16
NEG = -jnp.inf


def dot(a, b, dims):
    return lax.dot_general(a, b, (dims, ((), ())), preferred_element_type=f32)


def attention_step(allow_prev, q, do, k, v):
    scaling = 1.0 / math.sqrt(HEAD_DIM)
    log2e = math.log2(math.e)
    q4 = jnp.concatenate([q[:, h * HEAD_DIM : (h + 1) * HEAD_DIM] for h in range(GROUP)], 0)
    do4 = jnp.concatenate([do[:, h * HEAD_DIM : (h + 1) * HEAD_DIM] for h in range(GROUP)], 0)
    cols = GROUP * BLOCK
    s = dot(k, q4, ((1,), (1,)))
    row = lax.broadcasted_iota(jnp.int32, (BLOCK, cols), 0)
    col = lax.broadcasted_iota(jnp.int32, (BLOCK, cols), 1) % BLOCK
    s_prev = jnp.where(allow_prev, s[:BLOCK], NEG)
    s_own = jnp.where(row <= col, s[BLOCK:], NEG)
    s = jnp.concatenate([s_prev, s_own], 0)
    top = jnp.max(s, 0, keepdims=True)
    p = jnp.exp2((s - top) * (scaling * log2e))
    total = jnp.sum(p, 0, keepdims=True)
    dp = dot(v, do4, ((1,), (1,)))
    w = p * (1.0 / total)
    delta = jnp.sum(w * dp, 0, keepdims=True)
    ds = ((w * scaling) * (dp - delta)).astype(bf16)
    w_low = w.astype(bf16)
    dk = dot(ds, q4, ((1,), (0,)))
    dv = dot(w_low, do4, ((1,), (0,)))
    dq_t = dot(k, ds, ((0,), (0,))).astype(bf16)
    dq = jnp.concatenate(
        [dq_t[:, h * BLOCK : (h + 1) * BLOCK].T for h in range(GROUP)], 1
    )
    return dq, dk, dv


def own_kernel(blocks_ref, q_ref, do_ref, k_ref, v_ref, dq_ref, dk0_ref, dv0_ref, dk1_ref, dv1_ref):
    allow_prev = blocks_ref[3] != blocks_ref[2]
    dq, dk, dv = attention_step(allow_prev, q_ref[...], do_ref[...], k_ref[...], v_ref[...])
    dq_ref[...] = dq
    dk0_ref[...] = dk[:BLOCK]
    dv0_ref[...] = dv[:BLOCK]
    dk1_ref[...] = dk[BLOCK:]
    dv1_ref[...] = dv[BLOCK:]


def edge_kernel(
    blocks_ref, q_ref, do_ref, k_ref, v_ref, halo_ref, dk0_ref, dv0_ref, dq_in,
    dq_ref, back_k_ref, back_v_ref, dk_ref, dv_ref,
):
    del dq_in
    allow_prev = blocks_ref[1] != blocks_ref[0]
    g = pl.program_id(0)
    width = HEAD_DIM * KV_HEADS
    kh = halo_ref[:, pl.ds(pl.multiple_of(g * HEAD_DIM, HEAD_DIM), HEAD_DIM)]
    vh = halo_ref[:, pl.ds(pl.multiple_of(width + g * HEAD_DIM, HEAD_DIM), HEAD_DIM)]
    k = jnp.concatenate([kh, k_ref[...]], 0)
    v = jnp.concatenate([vh, v_ref[...]], 0)
    dq, dk, dv = attention_step(allow_prev, q_ref[...], do_ref[...], k, v)
    dq_ref[...] = dq
    back_k_ref[...] = dk[:BLOCK].astype(bf16)
    back_v_ref[...] = dv[:BLOCK].astype(bf16)
    dk_ref[...] = (dk[BLOCK:] + dk0_ref[...]).astype(bf16)
    dv_ref[...] = (dv[BLOCK:] + dv0_ref[...]).astype(bf16)


def join_kernel(dk1_ref, dv1_ref, back_ref, dk_in, dv_in, dk_ref, dv_ref):
    del dk_in, dv_in
    width = dk1_ref.shape[1]
    dk_ref[...] = (dk1_ref[...] + back_ref[:, :width].astype(f32)).astype(bf16)
    dv_ref[...] = (dv1_ref[...] + back_ref[:, width:].astype(f32)).astype(bf16)


def outer_kernel(recv_ref, cur_ref, moment_ref, nm_ref, send_ref):
    workers = recv_ref.shape[0]
    cur = cur_ref[...]
    drift = cur - recv_ref[0]
    for w in range(1, workers):
        drift += cur - recv_ref[w]
    drift = drift / workers
    nm = outer_moment * moment_ref[...] + drift
    nm_ref[...] = nm
    upd = (cur - outer_rate * (drift + outer_moment * nm)).astype(bf16)
    for w in range(workers):
        send_ref[w] = upd


def body(
    queries,
    key_states,
    value_states,
    output_grad,
    key_blocks,
    global_params,
    local_params,
    momentum,
    fragment,
):
    width = KV_HEADS * HEAD_DIM
    gwidth = GROUP * HEAD_DIM
    workers = lax.axis_size("worker")
    count = lax.axis_size("fsdp")
    span = LENGTH // queries.shape[0]
    ahead = [(i, i + 1) for i in range(count - 1) if (i + 1) % span]
    behind = [(j, i) for i, j in ahead]
    blocks = key_blocks.reshape(-1)

    halo = lax.ppermute(
        jnp.concatenate([key_states[BLOCK:], value_states[BLOCK:]], 1), "fsdp", ahead
    )

    frag_len = global_params.shape[1]
    share = frag_len // workers
    rows = share // LANES
    slot = fragment[0]
    recv = lax.all_to_all(
        local_params.reshape(workers, rows, LANES), "worker", 0, 0, tiled=True
    )

    smem = pl.BlockSpec(memory_space=pltpu.SMEM)
    vmem = pl.BlockSpec(memory_space=pltpu.VMEM)
    kv_struct = jax.ShapeDtypeStruct((BLOCK, width), f32)
    kv_spec = pl.BlockSpec((BLOCK, HEAD_DIM), lambda g: (0, g))
    est = pl.CostEstimate(
        flops=5 * 2 * HEADS * BLOCK * 2 * BLOCK * HEAD_DIM,
        bytes_accessed=2 * 1024 * 1024,
        transcendentals=HEADS * BLOCK * 2 * BLOCK,
    )
    dq, dk0, dv0, dk1, dv1 = pl.pallas_call(
        own_kernel,
        grid=(KV_HEADS,),
        in_specs=[
            smem,
            pl.BlockSpec((BLOCK, gwidth), lambda g: (1, g)),
            pl.BlockSpec((BLOCK, gwidth), lambda g: (1, g)),
            pl.BlockSpec((2 * BLOCK, HEAD_DIM), lambda g: (0, g)),
            pl.BlockSpec((2 * BLOCK, HEAD_DIM), lambda g: (0, g)),
        ],
        out_specs=[pl.BlockSpec((BLOCK, gwidth), lambda g: (1, g)), kv_spec, kv_spec, kv_spec, kv_spec],
        out_shape=[jax.ShapeDtypeStruct(queries.shape, bf16), kv_struct, kv_struct, kv_struct, kv_struct],
        cost_estimate=est,
        compiler_params=pltpu.CompilerParams(vmem_limit_bytes=16 << 20),
        name="attn_own",
    )(blocks, queries, output_grad, key_states, value_states)

    query_grad, back_k, back_v, key_grad, value_grad = pl.pallas_call(
        edge_kernel,
        grid=(KV_HEADS,),
        in_specs=[
            smem,
            pl.BlockSpec((BLOCK, gwidth), lambda g: (0, g)),
            pl.BlockSpec((BLOCK, gwidth), lambda g: (0, g)),
            kv_spec,
            kv_spec,
            vmem,
            kv_spec,
            kv_spec,
            pl.BlockSpec(memory_space=pl.ANY),
        ],
        out_specs=[
            pl.BlockSpec((BLOCK, gwidth), lambda g: (0, g)),
            kv_spec,
            kv_spec,
            kv_spec,
            kv_spec,
        ],
        out_shape=[
            jax.ShapeDtypeStruct(queries.shape, bf16),
            jax.ShapeDtypeStruct((BLOCK, width), bf16),
            jax.ShapeDtypeStruct((BLOCK, width), bf16),
            jax.ShapeDtypeStruct(key_states.shape, bf16),
            jax.ShapeDtypeStruct(value_states.shape, bf16),
        ],
        input_output_aliases={8: 0},
        cost_estimate=est,
        compiler_params=pltpu.CompilerParams(vmem_limit_bytes=16 << 20),
        name="attn_edge",
    )(blocks, queries, output_grad, key_states, value_states, halo, dk0, dv0, dq)

    back = lax.ppermute(jnp.concatenate([back_k, back_v], 1), "fsdp", behind)

    start = lax.axis_index("worker") * share
    cur = lax.dynamic_slice(global_params, (slot, start), (1, share)).reshape(rows, LANES)
    moment = lax.dynamic_index_in_dim(momentum, slot, 0, keepdims=False).reshape(rows, LANES)
    new_moment, send = pl.pallas_call(
        outer_kernel,
        out_shape=[
            jax.ShapeDtypeStruct((rows, LANES), f32),
            jax.ShapeDtypeStruct((workers, rows, LANES), bf16),
        ],
        in_specs=[vmem] * 3,
        out_specs=[vmem] * 2,
        compiler_params=pltpu.CompilerParams(vmem_limit_bytes=8 << 20),
        name="outer",
    )(recv, cur, moment)
    updated = lax.all_to_all(send, "worker", 0, 0, tiled=True).reshape(1, frag_len)
    picked = lax.broadcasted_iota(jnp.int32, global_params.shape, 0) == slot
    new_params = jnp.where(picked, updated.astype(f32), global_params)
    new_momentum = lax.dynamic_update_index_in_dim(
        momentum, new_moment.reshape(momentum.shape[1:]), slot, 0
    )

    half_spec = pl.BlockSpec((BLOCK, width), lambda i: (0, 0))
    key_grad, value_grad = pl.pallas_call(
        join_kernel,
        grid=(1,),
        in_specs=[
            half_spec,
            half_spec,
            vmem,
            pl.BlockSpec(memory_space=pl.ANY),
            pl.BlockSpec(memory_space=pl.ANY),
        ],
        out_specs=[pl.BlockSpec((BLOCK, width), lambda i: (1, 0))] * 2,
        out_shape=[
            jax.ShapeDtypeStruct(key_states.shape, bf16),
            jax.ShapeDtypeStruct(value_states.shape, bf16),
        ],
        input_output_aliases={3: 0, 4: 1},
        compiler_params=pltpu.CompilerParams(vmem_limit_bytes=8 << 20),
        name="join",
    )(dk1, dv1, back, key_grad, value_grad)
    return (query_grad, key_grad, value_grad, new_params, new_momentum)


def solution(mesh):
    placed = (
        P(("worker", "fsdp"), None),
        P(("worker", "fsdp"), None),
        P(("worker", "fsdp"), None),
        P(("worker", "fsdp"), None),
        P(("worker", "fsdp"), None),
        P(None, "fsdp"),
        P("worker", "fsdp"),
        P(None, "fsdp", "worker", None),
        P(),
    )
    return jax.shard_map(
        body,
        mesh=mesh,
        in_specs=placed,
        out_specs=(
            P(("worker", "fsdp"), None),
            P(("worker", "fsdp"), None),
            P(("worker", "fsdp"), None),
            P(None, "fsdp"),
            P(None, "fsdp", "worker", None),
        ),
        check_vma=False,
    )
```
